128 devices in a mesh: row: 8 (over x, core), col: 16 (over y, z).
Axes of the slice: x: 4, y: 4, z: 4, core: 2. Of those that a mesh axis runs over, the one named last changes fastest.
Arguments:
- density: float32 [768, 13, 4096], P(('row', 'col')), as said below
- pattern: int32 [768, 13], P(('row', 'col')), may hold values from 0 to 1, as said below
Outputs:
- purified: float32 [768, 13, 4096], P(('row', 'col'))
The draws below stay inside these ranges and needn't reach their ends.
Inputs may be any that keep to these rules, and one draw needn't show every extreme that they name: `pattern`: slot 6 is 1 in every row; slot s of block row i equals slot 12 - s of block row (i + s - 6) modulo 768. `density`: the block at slot s of block row i is the transpose of the block at slot 12 - s of block row (i + s - 6) modulo 768; blocks are zero where pattern is 0.
All inputs are finite; a program needn't handle non-finite values.
Results may differ from the reference program's by a relative error of at most 0.0001.
Values sent between devices are 32-bit elements; how exact they have to be, the bound alone decides.
No kernel may reach another device: no remote copies, remote signals or barrier semaphores. Data moves between devices by JAX's collectives and lax.ppermute only.
A program may use at most 128 MiB of HBM per device.

```python
import jax
import jax.numpy as jnp
from jax import lax

BLK = 64
HALF = 6
STEPS = 1
SLOTS = 13
NB = 768


def band_mask(key):
    edge_key = jax.random.fold_in(key, 11)
    edges = (jax.random.randint(edge_key, (NB, HALF), 0, 8) < 7).astype(jnp.int32)
    columns = []
    for slot in range(SLOTS):
        offset = slot - HALF
        if offset == 0:
            columns.append(jnp.ones((NB,), jnp.int32))
        elif offset > 0:
            columns.append(edges[:, offset - 1])
        else:
            columns.append(jnp.roll(edges[:, -offset - 1], -offset, axis=0))
    return jnp.stack(columns, axis=1)


def draw_pattern(key, part):
    return band_mask(key)


def draw_density(key, part):
    keep_mask = band_mask(key).astype(jnp.float32)
    raw_key = jax.random.fold_in(key, 23)
    raw = jax.random.normal(raw_key, (NB, SLOTS, BLK, BLK), jnp.float32)
    scales = jnp.ones((NB,), jnp.float32)
    sigma = 0.45 / (SLOTS * BLK) ** 0.5
    uppers = {}
    for offset in range(1, HALF + 1):
        factor = jnp.sqrt(jnp.roll(scales, -offset, axis=0))
        uppers[offset] = raw[:, HALF + offset] * factor[:, None, None]
    blocks = []
    for slot in range(SLOTS):
        offset = slot - HALF
        if offset == 0:
            middle = raw[:, HALF]
            blocks.append((middle + jnp.swapaxes(middle, 1, 2)) * 0.70710678)
        elif offset > 0:
            blocks.append(uppers[offset])
        else:
            blocks.append(jnp.swapaxes(jnp.roll(uppers[-offset], -offset, axis=0), 1, 2))
    matrix = sigma * jnp.stack(blocks, axis=1) * keep_mask[:, :, None, None]
    matrix = matrix.at[:, HALF].add(0.5 * jnp.eye(BLK, dtype=jnp.float32)[None])
    return matrix.reshape(NB, SLOTS, BLK * BLK)


def setup_inputs(seed: int = 0) -> dict:
    key_list = jax.random.split(jax.random.key(seed), 3)
    return {
        "density": draw_density(jax.random.fold_in(key_list[2], 71), 0),
        "pattern": draw_pattern(jax.random.fold_in(key_list[2], 71), 0),
    }


def band_product(left, right, keep_mask):
    result = jnp.zeros(left.shape, jnp.float32)
    for offset in range(-HALF, HALF + 1):
        shifted = jnp.roll(right, -offset, axis=0)
        first_slot = max(0, -offset)
        last_slot = min(SLOTS, SLOTS - offset)
        terms = jnp.einsum("nab,nsbc->nsac", left[:, offset + HALF], shifted[:, first_slot:last_slot], precision=lax.Precision.HIGHEST, preferred_element_type=jnp.float32)
        result = result.at[:, first_slot + offset:last_slot + offset].add(terms)
    return result * keep_mask


def reference(density, pattern):
    total = density.shape[0]
    current = density.reshape(total, SLOTS, BLK, BLK)
    keep_mask = pattern.astype(jnp.float32)[:, :, None, None]
    for iteration in range(STEPS):
        square = band_product(current, current, keep_mask)
        cube = band_product(square, current, keep_mask)
        current = 3.0 * square - 2.0 * cube
    return current.reshape(total, SLOTS, BLK * BLK)
```

```python
import jax
import jax.numpy as jnp
from jax import lax
from jax.experimental import pallas as pl
from jax.experimental.pallas import tpu as pltpu
from jax.sharding import PartitionSpec as P

BLK = 64
HALF = 6
SLOTS = 13
ROWS = 6
SUP = ROWS * BLK
LANES = 128
TILES = SUP // LANES
PACKED = 672
F32 = jnp.float32
BF16 = jnp.bfloat16


def lane_is_low(rows):
    return lax.broadcasted_iota(jnp.int32, (rows, LANES), 1) < BLK


def load_block(x_ref, row, slot):
    if slot < 0 or slot >= SLOTS:
        return jnp.zeros((BLK // 2, LANES), F32)
    return x_ref[row, slot, :].reshape(BLK // 2, LANES)


def even_odd_rows(left, right):
    low = lane_is_low(BLK // 2)
    even = jnp.where(low, left, pltpu.roll(right, BLK, 1))
    odd = jnp.where(low, pltpu.roll(left, BLK, 1), right)
    return even, odd


def store_pair(ref, lead, first_row, left, right):
    even, odd = even_odd_rows(left, right)
    ref[(*lead, pl.ds(first_row, BLK // 2, stride=2), slice(None))] = even
    ref[(*lead, pl.ds(first_row + 1, BLK // 2, stride=2), slice(None))] = odd


def split(x):
    hi = x.astype(BF16)
    return hi, (x - hi.astype(F32)).astype(BF16)


def dot(a, b):
    return jnp.dot(a, b, preferred_element_type=F32)


def dot3(ah, al, bh, bl):
    return dot(jnp.concatenate([ah, ah, al], 1), jnp.concatenate([bh, bl, bh], 0))


def mask_tile(pat_ref, row, tile):
    values = []
    for q in (2 * tile, 2 * tile + 1):
        slot = q - row
        values.append(pat_ref[row, slot].astype(F32) if 0 <= slot < SLOTS else jnp.float32(0.0))
    return jnp.where(lane_is_low(8), values[0], values[1])[:1]


def pack_kernel(x_ref, out_ref):
    first = 0
    for p in range(TILES):
        for row in (2 * p, 2 * p + 1):
            for q in range(p, TILES):
                if q == p and row % 2:
                    continue
                slot = 2 * q - row + HALF
                store_pair(out_ref, (), first, load_block(x_ref, row, slot), load_block(x_ref, row, slot + 1))
                first += BLK
    store_pair(out_ref, (), first, load_block(x_ref, 1, HALF), load_block(x_ref, 3, HALF))
    first += BLK
    out_ref[first : first + BLK // 2, :] = load_block(x_ref, 5, HALF)


def unpack(rec_ref, tri_ref):
    first = 0
    zeros = jnp.zeros((BLK, LANES), F32)
    for p in range(TILES):
        for row in (2 * p, 2 * p + 1):
            for q in range(p, TILES):
                if q == p and row % 2:
                    continue
                tri_ref[q, row * BLK : (row + 1) * BLK, :] = rec_ref[first : first + BLK, :]
                first += BLK
    corner = rec_ref[first : first + BLK, :]
    low = lane_is_low(BLK)
    tri_ref[0, BLK : 2 * BLK, :] = jnp.where(low, zeros, pltpu.roll(corner, BLK, 1))
    tri_ref[1, 3 * BLK : 4 * BLK, :] = jnp.where(low, zeros, corner)
    first += BLK
    last = rec_ref[first : first + BLK // 2, :]
    store_pair(tri_ref, (2,), 5 * BLK, jnp.zeros((BLK // 2, LANES), F32), last)


def unpack_split(rec_ref, tri_ref, hi_ref, lo_ref):
    unpack(rec_ref, tri_ref)
    shape = (LANES, LANES)
    corner = (lax.broadcasted_iota(jnp.int32, shape, 0) >= BLK) & (lax.broadcasted_iota(jnp.int32, shape, 1) < BLK)
    for p in range(TILES):
        for q in range(p, TILES):
            tile = tri_ref[q, p * LANES : (p + 1) * LANES, :]
            turned = tile.T
            here = (slice(p * LANES, (p + 1) * LANES), slice(q * LANES, (q + 1) * LANES))
            there = (here[1], here[0])
            if p == q:
                hi_ref[here], lo_ref[here] = split(jnp.where(corner, turned, tile))
            else:
                hi_ref[here], lo_ref[here] = split(tile)
                hi_ref[there], lo_ref[there] = split(turned)


def local_kernel(pat_ref, x_ref, xh_ref, xl_ref, th_ref, tl_ref, base_ref, part_ref, side_ref, nat_ref, sqh_ref, sql_ref):
    for row in range(ROWS):
        for tile in range(3 * TILES):
            slot = 2 * tile - row
            store_pair(nat_ref, (tile,), row * BLK, load_block(x_ref, row, slot), load_block(x_ref, row, slot + 1))
    for tile in range(3 * TILES):
        cols = slice(tile * LANES, (tile + 1) * LANES)
        xh_ref[:, cols], xl_ref[:, cols] = split(nat_ref[tile])
        th_ref[cols, :], tl_ref[cols, :] = split(nat_ref[tile].T)
    square = dot3(xh_ref[...], xl_ref[...], th_ref[...], tl_ref[...])
    for row in range(ROWS):
        rows = slice(row * BLK, (row + 1) * BLK)
        for tile in range(TILES):
            cols = slice(tile * LANES, (tile + 1) * LANES)
            kept = square[rows, cols] * mask_tile(pat_ref, row, TILES + tile)
            base_ref[rows, cols] = kept
            sqh_ref[rows, cols], sql_ref[rows, cols] = split(kept)
    dh, dl = xh_ref[:, SUP : 2 * SUP], xl_ref[:, SUP : 2 * SUP]
    for side, first in ((0, 0), (1, 2 * SUP)):
        cols = slice(first, first + SUP)
        part_ref[side] = dot3(dh, dl, xh_ref[:, cols], xl_ref[:, cols])
        side_ref[side] = dot3(sqh_ref[...], sql_ref[...], xh_ref[:, cols], xl_ref[:, cols])
    cube = dot3(sqh_ref[...], sql_ref[...], dh, dl)
    base_ref[...] = 3.0 * base_ref[...] - 2.0 * cube


def finish_kernel(
    pat_ref, prev_ref, next_ref, xh_ref, xl_ref, th_ref, tl_ref, base_ref, part_ref, side_ref,
    out_ref, tri_ref, dh_ref, dl_ref, eh_ref, el_ref, nat_ref,
):
    for side, rec_ref in ((0, prev_ref), (1, next_ref)):
        unpack_split(rec_ref, tri_ref.at[side], dh_ref.at[side], dl_ref.at[side])
    for side in (0, 1):
        cols = slice(2 * side * SUP, (2 * side + 1) * SUP)
        edge = part_ref[side] + dot3(xh_ref[:, cols], xl_ref[:, cols], dh_ref[side], dl_ref[side])
        for row in range(ROWS):
            rows = slice(row * BLK, (row + 1) * BLK)
            for t in range(TILES):
                tile = 2 * side * TILES + t
                lanes = slice(t * LANES, (t + 1) * LANES)
                kept = edge[rows, lanes] * mask_tile(pat_ref, row, tile)
                nat_ref[tile, rows, :] = 3.0 * kept
                lanes = slice(side * SUP + t * LANES, side * SUP + (t + 1) * LANES)
                eh_ref[rows, lanes], el_ref[rows, lanes] = split(kept)
    for side in (0, 1):
        cols = slice(side * SUP, (side + 1) * SUP)
        cube = side_ref[side] + dot3(eh_ref[:, cols], el_ref[:, cols], dh_ref[side], dl_ref[side])
        for t in range(TILES):
            tile = 2 * side * TILES + t
            nat_ref[tile] = nat_ref[tile] - 2.0 * cube[:, t * LANES : (t + 1) * LANES]
    turned_h = jnp.concatenate([th_ref[:SUP, :], th_ref[2 * SUP :, :]], 0)
    turned_l = jnp.concatenate([tl_ref[:SUP, :], tl_ref[2 * SUP :, :]], 0)
    cube = dot3(eh_ref[...], el_ref[...], turned_h, turned_l)
    for t in range(TILES):
        lanes = slice(t * LANES, (t + 1) * LANES)
        nat_ref[TILES + t] = base_ref[:, lanes] - 2.0 * cube[:, lanes]
    for row in range(ROWS):
        for tile in range(row // 2, (row + SLOTS - 1) // 2 + 1):
            mask = mask_tile(pat_ref, row, tile)
            even = nat_ref[tile, pl.ds(row * BLK, BLK // 2, stride=2), :] * mask
            odd = nat_ref[tile, pl.ds(row * BLK + 1, BLK // 2, stride=2), :] * mask
            left, right = even_odd_rows(even, odd)
            for slot, block in ((2 * tile - row, left), (2 * tile + 1 - row, right)):
                if 0 <= slot < SLOTS:
                    out_ref[row, slot, :] = block.reshape(BLK * BLK)


def from_behind(x, by):
    axes = ("row", "col")
    length = lax.axis_size(axes)
    return lax.ppermute(x, axes, [(i, (i + by) % length) for i in range(length)])


def shards(density, pattern):
    smem = pl.BlockSpec(memory_space=pltpu.SMEM)
    vmem = pl.BlockSpec(memory_space=pltpu.VMEM)
    packed = pl.pallas_call(
        pack_kernel, out_shape=jax.ShapeDtypeStruct((PACKED, LANES), F32), name="pack"
    )(density)
    prev = from_behind(packed, 1)
    following = from_behind(packed, -1)
    local = pl.pallas_call(
        local_kernel,
        name="local",
        in_specs=[smem, vmem],
        out_specs=[vmem] * 7,
        out_shape=[
            jax.ShapeDtypeStruct((SUP, 3 * SUP), BF16),
            jax.ShapeDtypeStruct((SUP, 3 * SUP), BF16),
            jax.ShapeDtypeStruct((3 * SUP, SUP), BF16),
            jax.ShapeDtypeStruct((3 * SUP, SUP), BF16),
            jax.ShapeDtypeStruct((SUP, SUP), F32),
            jax.ShapeDtypeStruct((2, SUP, SUP), F32),
            jax.ShapeDtypeStruct((2, SUP, SUP), F32),
        ],
        scratch_shapes=[
            pltpu.VMEM((3 * TILES, SUP, LANES), F32),
            pltpu.VMEM((SUP, SUP), BF16),
            pltpu.VMEM((SUP, SUP), BF16),
        ],
    )(pattern, density)
    return pl.pallas_call(
        finish_kernel,
        name="finish",
        in_specs=[smem] + [vmem] * 9,
        out_specs=vmem,
        out_shape=jax.ShapeDtypeStruct((ROWS, SLOTS, BLK * BLK), F32),
        scratch_shapes=[
            pltpu.VMEM((2, TILES, SUP, LANES), F32),
            pltpu.VMEM((2, SUP, SUP), BF16),
            pltpu.VMEM((2, SUP, SUP), BF16),
            pltpu.VMEM((SUP, 2 * SUP), BF16),
            pltpu.VMEM((SUP, 2 * SUP), BF16),
            pltpu.VMEM((3 * TILES, SUP, LANES), F32),
        ],
    )(pattern, prev, following, *local)


def solution(mesh):
    return jax.shard_map(
        shards,
        mesh=mesh,
        in_specs=(P(("row", "col"), None, None), P(("row", "col"), None)),
        out_specs=P(("row", "col"), None, None),
        check_vma=False,
    )
```

```python
import jax
import jax.numpy as jnp
from jax import lax
from jax.experimental import pallas as pl
from jax.experimental.pallas import tpu as pltpu
from jax.sharding import PartitionSpec as P

BLK = 64
HALF = 6
SLOTS = 13
ROWS = 6
SUP = ROWS * BLK
LANES = 128
TILES = SUP // LANES
PACKED = 672
F32 = jnp.float32
BF16 = jnp.bfloat16
SMALL = pltpu.CompilerParams(vmem_limit_bytes=24 << 20)


def lane_is_low(rows):
    return lax.broadcasted_iota(jnp.int32, (rows, LANES), 1) < BLK


def load_block(x_ref, row, slot):
    if slot < 0 or slot >= SLOTS:
        return jnp.zeros((BLK // 2, LANES), F32)
    return x_ref[row, slot, :].reshape(BLK // 2, LANES)


def even_odd_rows(left, right):
    low = lane_is_low(BLK // 2)
    even = jnp.where(low, left, pltpu.roll(right, BLK, 1))
    odd = jnp.where(low, pltpu.roll(left, BLK, 1), right)
    return even, odd


def store_pair(ref, lead, first_row, left, right):
    even, odd = even_odd_rows(left, right)
    ref[(*lead, pl.ds(first_row, BLK // 2, stride=2), slice(None))] = even
    ref[(*lead, pl.ds(first_row + 1, BLK // 2, stride=2), slice(None))] = odd


def split(x):
    hi = x.astype(BF16)
    return hi, (x - hi.astype(F32)).astype(BF16)


def dot(a, b):
    return jnp.dot(a, b, preferred_element_type=F32)


def dot3(ah, al, bh, bl):
    return dot(jnp.concatenate([ah, ah, al], 1), jnp.concatenate([bh, bl, bh], 0))


def mask_tile(pat_ref, row, tile):
    values = []
    for q in (2 * tile, 2 * tile + 1):
        slot = q - row
        values.append(pat_ref[row, slot].astype(F32) if 0 <= slot < SLOTS else jnp.float32(0.0))
    return jnp.where(lane_is_low(8), values[0], values[1])[:1]


def pack_kernel(x_ref, out_ref):
    first = 0
    for p in range(TILES):
        for row in (2 * p, 2 * p + 1):
            for q in range(p, TILES):
                if q == p and row % 2:
                    continue
                slot = 2 * q - row + HALF
                store_pair(out_ref, (), first, load_block(x_ref, row, slot), load_block(x_ref, row, slot + 1))
                first += BLK
    store_pair(out_ref, (), first, load_block(x_ref, 1, HALF), load_block(x_ref, 3, HALF))
    first += BLK
    out_ref[first : first + BLK // 2, :] = load_block(x_ref, 5, HALF)


def unpack(rec_ref, tri_ref):
    first = 0
    zeros = jnp.zeros((BLK, LANES), F32)
    for p in range(TILES):
        for row in (2 * p, 2 * p + 1):
            for q in range(p, TILES):
                if q == p and row % 2:
                    continue
                tri_ref[q, row * BLK : (row + 1) * BLK, :] = rec_ref[first : first + BLK, :]
                first += BLK
    corner = rec_ref[first : first + BLK, :]
    low = lane_is_low(BLK)
    tri_ref[0, BLK : 2 * BLK, :] = jnp.where(low, zeros, pltpu.roll(corner, BLK, 1))
    tri_ref[1, 3 * BLK : 4 * BLK, :] = jnp.where(low, zeros, corner)
    first += BLK
    last = rec_ref[first : first + BLK // 2, :]
    store_pair(tri_ref, (2,), 5 * BLK, jnp.zeros((BLK // 2, LANES), F32), last)


def unpack_split(rec_ref, tri_ref, hi_ref, lo_ref):
    unpack(rec_ref, tri_ref)
    shape = (LANES, LANES)
    corner = (lax.broadcasted_iota(jnp.int32, shape, 0) >= BLK) & (lax.broadcasted_iota(jnp.int32, shape, 1) < BLK)
    for p in range(TILES):
        for q in range(p, TILES):
            tile = tri_ref[q, p * LANES : (p + 1) * LANES, :]
            turned = tile.T
            here = (slice(p * LANES, (p + 1) * LANES), slice(q * LANES, (q + 1) * LANES))
            there = (here[1], here[0])
            if p == q:
                hi_ref[here], lo_ref[here] = split(jnp.where(corner, turned, tile))
            else:
                hi_ref[here], lo_ref[here] = split(tile)
                hi_ref[there], lo_ref[there] = split(turned)


def local_kernel(pat_ref, x_ref, xh_ref, xl_ref, th_ref, tl_ref, base_ref, part_ref, side_ref, nat_ref, sqh_ref, sql_ref):
    for row in range(ROWS):
        for tile in range(3 * TILES):
            slot = 2 * tile - row
            store_pair(nat_ref, (tile,), row * BLK, load_block(x_ref, row, slot), load_block(x_ref, row, slot + 1))
    for tile in range(3 * TILES):
        cols = slice(tile * LANES, (tile + 1) * LANES)
        xh_ref[:, cols], xl_ref[:, cols] = split(nat_ref[tile])
        th_ref[cols, :], tl_ref[cols, :] = split(nat_ref[tile].T)
    square = dot3(xh_ref[...], xl_ref[...], th_ref[...], tl_ref[...])
    for row in range(ROWS):
        rows = slice(row * BLK, (row + 1) * BLK)
        for tile in range(TILES):
            cols = slice(tile * LANES, (tile + 1) * LANES)
            kept = square[rows, cols] * mask_tile(pat_ref, row, TILES + tile)
            base_ref[rows, cols] = kept
            sqh_ref[rows, cols], sql_ref[rows, cols] = split(kept)
    dh, dl = xh_ref[:, SUP : 2 * SUP], xl_ref[:, SUP : 2 * SUP]
    for side, first in ((0, 0), (1, 2 * SUP)):
        cols = slice(first, first + SUP)
        part_ref[side] = dot3(dh, dl, xh_ref[:, cols], xl_ref[:, cols])
        side_ref[side] = dot3(sqh_ref[...], sql_ref[...], xh_ref[:, cols], xl_ref[:, cols])
    cube = dot3(sqh_ref[...], sql_ref[...], dh, dl)
    base_ref[...] = 3.0 * base_ref[...] - 2.0 * cube


def finish_kernel(
    pat_ref, prev_ref, next_ref, xh_ref, xl_ref, th_ref, tl_ref, base_ref, part_ref, side_ref,
    out_ref, tri_ref, dh_ref, dl_ref, eh_ref, el_ref, nat_ref,
):
    for side, rec_ref in ((0, prev_ref), (1, next_ref)):
        unpack_split(rec_ref, tri_ref.at[side], dh_ref.at[side], dl_ref.at[side])
    for side in (0, 1):
        cols = slice(2 * side * SUP, (2 * side + 1) * SUP)
        edge = part_ref[side] + dot3(xh_ref[:, cols], xl_ref[:, cols], dh_ref[side], dl_ref[side])
        for row in range(ROWS):
            rows = slice(row * BLK, (row + 1) * BLK)
            for t in range(TILES):
                tile = 2 * side * TILES + t
                lanes = slice(t * LANES, (t + 1) * LANES)
                kept = edge[rows, lanes] * mask_tile(pat_ref, row, tile)
                nat_ref[tile, rows, :] = 3.0 * kept
                lanes = slice(side * SUP + t * LANES, side * SUP + (t + 1) * LANES)
                eh_ref[rows, lanes], el_ref[rows, lanes] = split(kept)
    for side in (0, 1):
        cols = slice(side * SUP, (side + 1) * SUP)
        cube = side_ref[side] + dot3(eh_ref[:, cols], el_ref[:, cols], dh_ref[side], dl_ref[side])
        for t in range(TILES):
            tile = 2 * side * TILES + t
            nat_ref[tile] = nat_ref[tile] - 2.0 * cube[:, t * LANES : (t + 1) * LANES]
    turned_h = jnp.concatenate([th_ref[:SUP, :], th_ref[2 * SUP :, :]], 0)
    turned_l = jnp.concatenate([tl_ref[:SUP, :], tl_ref[2 * SUP :, :]], 0)
    cube = dot3(eh_ref[...], el_ref[...], turned_h, turned_l)
    for t in range(TILES):
        lanes = slice(t * LANES, (t + 1) * LANES)
        nat_ref[TILES + t] = base_ref[:, lanes] - 2.0 * cube[:, lanes]
    for row in range(ROWS):
        for tile in range(row // 2, (row + SLOTS - 1) // 2 + 1):
            mask = mask_tile(pat_ref, row, tile)
            even = nat_ref[tile, pl.ds(row * BLK, BLK // 2, stride=2), :] * mask
            odd = nat_ref[tile, pl.ds(row * BLK + 1, BLK // 2, stride=2), :] * mask
            left, right = even_odd_rows(even, odd)
            for slot, block in ((2 * tile - row, left), (2 * tile + 1 - row, right)):
                if 0 <= slot < SLOTS:
                    out_ref[row, slot, :] = block.reshape(BLK * BLK)


def from_behind(x, by):
    axes = ("row", "col")
    length = lax.axis_size(axes)
    return lax.ppermute(x, axes, [(i, (i + by) % length) for i in range(length)])


def on_chip(x):
    return pltpu.with_memory_space_constraint(x, pltpu.VMEM)


def shards(density, pattern):
    smem = pl.BlockSpec(memory_space=pltpu.SMEM)
    vmem = pl.BlockSpec(memory_space=pltpu.VMEM)
    packed = pl.pallas_call(pack_kernel, out_specs=vmem, out_shape=pltpu.VMEM((PACKED, LANES), F32), name="pack", compiler_params=SMALL)(density)
    prev = from_behind(packed, 1)
    following = from_behind(packed, -1)
    local = pl.pallas_call(
        local_kernel,
        name="local",
        compiler_params=SMALL,
        in_specs=[smem, vmem],
        out_specs=[vmem] * 7,
        out_shape=[
            pltpu.VMEM((SUP, 3 * SUP), BF16),
            pltpu.VMEM((SUP, 3 * SUP), BF16),
            pltpu.VMEM((3 * SUP, SUP), BF16),
            pltpu.VMEM((3 * SUP, SUP), BF16),
            pltpu.VMEM((SUP, SUP), F32),
            pltpu.VMEM((2, SUP, SUP), F32),
            pltpu.VMEM((2, SUP, SUP), F32),
        ],
        scratch_shapes=[
            pltpu.VMEM((3 * TILES, SUP, LANES), F32),
            pltpu.VMEM((SUP, SUP), BF16),
            pltpu.VMEM((SUP, SUP), BF16),
        ],
    )(pattern, density)
    return pl.pallas_call(
        finish_kernel,
        name="finish",
        compiler_params=SMALL,
        in_specs=[smem] + [vmem] * 9,
        out_specs=vmem,
        out_shape=jax.ShapeDtypeStruct((ROWS, SLOTS, BLK * BLK), F32),
        scratch_shapes=[
            pltpu.VMEM((2, TILES, SUP, LANES), F32),
            pltpu.VMEM((2, SUP, SUP), BF16),
            pltpu.VMEM((2, SUP, SUP), BF16),
            pltpu.VMEM((SUP, 2 * SUP), BF16),
            pltpu.VMEM((SUP, 2 * SUP), BF16),
            pltpu.VMEM((3 * TILES, SUP, LANES), F32),
        ],
    )(pattern, *(on_chip(x) for x in (prev, following, *local)))


def solution(mesh):
    return jax.shard_map(
        shards,
        mesh=mesh,
        in_specs=(P(("row", "col"), None, None), P(("row", "col"), None)),
        out_specs=P(("row", "col"), None, None),
        check_vma=False,
    )
```

```python
import jax
import jax.numpy as jnp
from jax import lax
from jax.experimental import pallas as pl
from jax.experimental.pallas import tpu as pltpu
from jax.sharding import PartitionSpec as P

BLK = 64
HALF = 6
SLOTS = 13
ROWS = 6
SUP = ROWS * BLK
LANES = 128
TILES = SUP // LANES
PACKED = 672
F32 = jnp.float32
BF16 = jnp.bfloat16
SMALL = pltpu.CompilerParams(vmem_limit_bytes=24 << 20)


def lane_is_low(rows):
    return lax.broadcasted_iota(jnp.int32, (rows, LANES), 1) < BLK


def load_block(x_ref, row, slot):
    if slot < 0 or slot >= SLOTS:
        return jnp.zeros((BLK // 2, LANES), F32)
    return x_ref[row, slot, :].reshape(BLK // 2, LANES)


def even_odd_rows(left, right):
    low = lane_is_low(BLK // 2)
    even = jnp.where(low, left, pltpu.roll(right, BLK, 1))
    odd = jnp.where(low, pltpu.roll(left, BLK, 1), right)
    return even, odd


def store_pair(ref, lead, first_row, left, right):
    even, odd = even_odd_rows(left, right)
    ref[(*lead, pl.ds(first_row, BLK // 2, stride=2), slice(None))] = even
    ref[(*lead, pl.ds(first_row + 1, BLK // 2, stride=2), slice(None))] = odd


def split(x):
    hi = x.astype(BF16)
    return hi, (x - hi.astype(F32)).astype(BF16)


def dot(a, b):
    return jnp.dot(a, b, preferred_element_type=F32)


def dot3(ah, al, bh, bl):
    return dot(jnp.concatenate([ah, ah, al], 1), jnp.concatenate([bh, bl, bh], 0))


def mask_tile(pat_ref, row, tile):
    values = []
    for q in (2 * tile, 2 * tile + 1):
        slot = q - row
        values.append(pat_ref[row, slot].astype(F32) if 0 <= slot < SLOTS else jnp.float32(0.0))
    return jnp.where(lane_is_low(8), values[0], values[1])[:1]


def pack_kernel(hbm_ref, out_ref, x_ref, sems):
    copies = [pltpu.make_async_copy(hbm_ref.at[row], x_ref.at[row], sems.at[row]) for row in range(ROWS)]
    for copy in copies:
        copy.start()
    for copy in copies:
        copy.wait()
    first = 0
    for p in range(TILES):
        for row in (2 * p, 2 * p + 1):
            for q in range(p, TILES):
                if q == p and row % 2:
                    continue
                slot = 2 * q - row + HALF
                store_pair(out_ref, (), first, load_block(x_ref, row, slot), load_block(x_ref, row, slot + 1))
                first += BLK
    store_pair(out_ref, (), first, load_block(x_ref, 1, HALF), load_block(x_ref, 3, HALF))
    first += BLK
    out_ref[first : first + BLK // 2, :] = load_block(x_ref, 5, HALF)


def unpack(rec_ref, tri_ref):
    first = 0
    zeros = jnp.zeros((BLK, LANES), F32)
    for p in range(TILES):
        for row in (2 * p, 2 * p + 1):
            for q in range(p, TILES):
                if q == p and row % 2:
                    continue
                tri_ref[q, row * BLK : (row + 1) * BLK, :] = rec_ref[first : first + BLK, :]
                first += BLK
    corner = rec_ref[first : first + BLK, :]
    low = lane_is_low(BLK)
    tri_ref[0, BLK : 2 * BLK, :] = jnp.where(low, zeros, pltpu.roll(corner, BLK, 1))
    tri_ref[1, 3 * BLK : 4 * BLK, :] = jnp.where(low, zeros, corner)
    first += BLK
    last = rec_ref[first : first + BLK // 2, :]
    store_pair(tri_ref, (2,), 5 * BLK, jnp.zeros((BLK // 2, LANES), F32), last)


def unpack_split(rec_ref, tri_ref, hi_ref, lo_ref):
    unpack(rec_ref, tri_ref)
    shape = (LANES, LANES)
    corner = (lax.broadcasted_iota(jnp.int32, shape, 0) >= BLK) & (lax.broadcasted_iota(jnp.int32, shape, 1) < BLK)
    for p in range(TILES):
        for q in range(p, TILES):
            tile = tri_ref[q, p * LANES : (p + 1) * LANES, :]
            turned = tile.T
            here = (slice(p * LANES, (p + 1) * LANES), slice(q * LANES, (q + 1) * LANES))
            there = (here[1], here[0])
            if p == q:
                hi_ref[here], lo_ref[here] = split(jnp.where(corner, turned, tile))
            else:
                hi_ref[here], lo_ref[here] = split(tile)
                hi_ref[there], lo_ref[there] = split(turned)


def local_kernel(pat_ref, x_ref, xh_ref, xl_ref, th_ref, tl_ref, base_ref, part_ref, side_ref, nat_ref, sqh_ref, sql_ref):
    for row in range(ROWS):
        for tile in range(3 * TILES):
            slot = 2 * tile - row
            store_pair(nat_ref, (tile,), row * BLK, load_block(x_ref, row, slot), load_block(x_ref, row, slot + 1))
    for tile in range(3 * TILES):
        cols = slice(tile * LANES, (tile + 1) * LANES)
        xh_ref[:, cols], xl_ref[:, cols] = split(nat_ref[tile])
        th_ref[cols, :], tl_ref[cols, :] = split(nat_ref[tile].T)
    square = dot3(xh_ref[...], xl_ref[...], th_ref[...], tl_ref[...])
    for row in range(ROWS):
        rows = slice(row * BLK, (row + 1) * BLK)
        for tile in range(TILES):
            cols = slice(tile * LANES, (tile + 1) * LANES)
            kept = square[rows, cols] * mask_tile(pat_ref, row, TILES + tile)
            base_ref[rows, cols] = kept
            sqh_ref[rows, cols], sql_ref[rows, cols] = split(kept)
    dh, dl = xh_ref[:, SUP : 2 * SUP], xl_ref[:, SUP : 2 * SUP]
    for side, first in ((0, 0), (1, 2 * SUP)):
        cols = slice(first, first + SUP)
        part_ref[side] = dot3(dh, dl, xh_ref[:, cols], xl_ref[:, cols])
        side_ref[side] = dot3(sqh_ref[...], sql_ref[...], xh_ref[:, cols], xl_ref[:, cols])
    cube = dot3(sqh_ref[...], sql_ref[...], dh, dl)
    base_ref[...] = 3.0 * base_ref[...] - 2.0 * cube


def finish_kernel(
    pat_ref, prev_ref, next_ref, xh_ref, xl_ref, th_ref, tl_ref, base_ref, part_ref, side_ref,
    out_ref, tri_ref, dh_ref, dl_ref, eh_ref, el_ref, nat_ref,
):
    for side, rec_ref in ((0, prev_ref), (1, next_ref)):
        unpack_split(rec_ref, tri_ref.at[side], dh_ref.at[side], dl_ref.at[side])
    for side in (0, 1):
        cols = slice(2 * side * SUP, (2 * side + 1) * SUP)
        edge = part_ref[side] + dot3(xh_ref[:, cols], xl_ref[:, cols], dh_ref[side], dl_ref[side])
        for row in range(ROWS):
            rows = slice(row * BLK, (row + 1) * BLK)
            for t in range(TILES):
                tile = 2 * side * TILES + t
                lanes = slice(t * LANES, (t + 1) * LANES)
                kept = edge[rows, lanes] * mask_tile(pat_ref, row, tile)
                nat_ref[tile, rows, :] = 3.0 * kept
                lanes = slice(side * SUP + t * LANES, side * SUP + (t + 1) * LANES)
                eh_ref[rows, lanes], el_ref[rows, lanes] = split(kept)
    for side in (0, 1):
        cols = slice(side * SUP, (side + 1) * SUP)
        cube = side_ref[side] + dot3(eh_ref[:, cols], el_ref[:, cols], dh_ref[side], dl_ref[side])
        for t in range(TILES):
            tile = 2 * side * TILES + t
            nat_ref[tile] = nat_ref[tile] - 2.0 * cube[:, t * LANES : (t + 1) * LANES]
    turned_h = jnp.concatenate([th_ref[:SUP, :], th_ref[2 * SUP :, :]], 0)
    turned_l = jnp.concatenate([tl_ref[:SUP, :], tl_ref[2 * SUP :, :]], 0)
    cube = dot3(eh_ref[...], el_ref[...], turned_h, turned_l)
    for t in range(TILES):
        lanes = slice(t * LANES, (t + 1) * LANES)
        nat_ref[TILES + t] = base_ref[:, lanes] - 2.0 * cube[:, lanes]
    for row in range(ROWS):
        for tile in range(row // 2, (row + SLOTS - 1) // 2 + 1):
            mask = mask_tile(pat_ref, row, tile)
            even = nat_ref[tile, pl.ds(row * BLK, BLK // 2, stride=2), :] * mask
            odd = nat_ref[tile, pl.ds(row * BLK + 1, BLK // 2, stride=2), :] * mask
            left, right = even_odd_rows(even, odd)
            for slot, block in ((2 * tile - row, left), (2 * tile + 1 - row, right)):
                if 0 <= slot < SLOTS:
                    out_ref[row, slot, :] = block.reshape(BLK * BLK)


def from_behind(x, by):
    axes = ("row", "col")
    length = lax.axis_size(axes)
    return lax.ppermute(x, axes, [(i, (i + by) % length) for i in range(length)])


def on_chip(x):
    return pltpu.with_memory_space_constraint(x, pltpu.VMEM)


def shards(density, pattern):
    smem = pl.BlockSpec(memory_space=pltpu.SMEM)
    vmem = pl.BlockSpec(memory_space=pltpu.VMEM)
    packed, density = pl.pallas_call(
        pack_kernel,
        name="pack",
        compiler_params=SMALL,
        in_specs=[pl.BlockSpec(memory_space=pltpu.HBM)],
        out_specs=[vmem] * 2,
        out_shape=[pltpu.VMEM((PACKED, LANES), F32), pltpu.VMEM((ROWS, SLOTS, BLK * BLK), F32)],
        scratch_shapes=[pltpu.SemaphoreType.DMA((ROWS,))],
    )(pltpu.with_memory_space_constraint(density, pltpu.HBM))
    density = on_chip(density)
    following = from_behind(packed, -1)
    prev = from_behind(packed, 1)
    local = pl.pallas_call(
        local_kernel,
        name="local",
        compiler_params=SMALL,
        in_specs=[smem, vmem],
        out_specs=[vmem] * 7,
        out_shape=[
            pltpu.VMEM((SUP, 3 * SUP), BF16),
            pltpu.VMEM((SUP, 3 * SUP), BF16),
            pltpu.VMEM((3 * SUP, SUP), BF16),
            pltpu.VMEM((3 * SUP, SUP), BF16),
            pltpu.VMEM((SUP, SUP), F32),
            pltpu.VMEM((2, SUP, SUP), F32),
            pltpu.VMEM((2, SUP, SUP), F32),
        ],
        scratch_shapes=[
            pltpu.VMEM((3 * TILES, SUP, LANES), F32),
            pltpu.VMEM((SUP, SUP), BF16),
            pltpu.VMEM((SUP, SUP), BF16),
        ],
    )(pattern, density)
    return pl.pallas_call(
        finish_kernel,
        name="finish",
        compiler_params=SMALL,
        in_specs=[smem] + [vmem] * 9,
        out_specs=vmem,
        out_shape=jax.ShapeDtypeStruct((ROWS, SLOTS, BLK * BLK), F32),
        scratch_shapes=[
            pltpu.VMEM((2, TILES, SUP, LANES), F32),
            pltpu.VMEM((2, SUP, SUP), BF16),
            pltpu.VMEM((2, SUP, SUP), BF16),
            pltpu.VMEM((SUP, 2 * SUP), BF16),
            pltpu.VMEM((SUP, 2 * SUP), BF16),
            pltpu.VMEM((3 * TILES, SUP, LANES), F32),
        ],
    )(pattern, *(on_chip(x) for x in (prev, following, *local)))


def solution(mesh):
    return jax.shard_map(
        shards,
        mesh=mesh,
        in_specs=(P(("row", "col"), None, None), P(("row", "col"), None)),
        out_specs=P(("row", "col"), None, None),
        check_vma=False,
    )
```

```python
import jax
import jax.numpy as jnp
from jax import lax
from jax.experimental import pallas as pl
from jax.experimental.pallas import tpu as pltpu
from jax.sharding import PartitionSpec as P

BLK = 64
HALF = 6
SLOTS = 13
ROWS = 6
SUP = ROWS * BLK
LANES = 128
TILES = SUP // LANES
F32 = jnp.float32
BF16 = jnp.bfloat16
SMALL = pltpu.CompilerParams(vmem_limit_bytes=24 << 20)


def lane_is_low(rows):
    return lax.broadcasted_iota(jnp.int32, (rows, LANES), 1) < BLK


def load_block(x_ref, row, slot):
    if slot < 0 or slot >= SLOTS:
        return jnp.zeros((BLK // 2, LANES), F32)
    return x_ref[row, slot, :].reshape(BLK // 2, LANES)


def even_odd_rows(left, right):
    low = lane_is_low(BLK // 2)
    even = jnp.where(low, left, pltpu.roll(right, BLK, 1))
    odd = jnp.where(low, pltpu.roll(left, BLK, 1), right)
    return even, odd


def store_pair(ref, lead, first_row, left, right):
    even, odd = even_odd_rows(left, right)
    ref[(*lead, pl.ds(first_row, BLK // 2, stride=2), slice(None))] = even
    ref[(*lead, pl.ds(first_row + 1, BLK // 2, stride=2), slice(None))] = odd


def split(x):
    hi = x.astype(BF16)
    return hi, (x - hi.astype(F32)).astype(BF16)


def dot(a, b):
    return jnp.dot(a, b, preferred_element_type=F32)


def dot3(ah, al, bh, bl):
    return dot(jnp.concatenate([ah, ah, al], 1), jnp.concatenate([bh, bl, bh], 0))


def mask_tile(pat_ref, row, tile):
    values = []
    for q in (2 * tile, 2 * tile + 1):
        slot = q - row
        values.append(pat_ref[row, slot].astype(F32) if 0 <= slot < SLOTS else jnp.float32(0.0))
    return jnp.where(lane_is_low(8), values[0], values[1])[:1]


def packed_rows():
    first = {}
    for p in range(TILES):
        for row in (2 * p, 2 * p + 1):
            for q in range(p + row % 2, TILES):
                first[row, q] = BLK * len(first)
    return first


FIRST = packed_rows()
DIAGONALS = BLK * len(FIRST)
PACKED = DIAGONALS + 8


def pack_kernel(hbm_ref, out_ref, x_ref, sems):
    copies = [pltpu.make_async_copy(hbm_ref.at[row], x_ref.at[row], sems.at[row]) for row in range(ROWS)]
    for copy in copies:
        copy.start()
    for copy in copies:
        copy.wait()
    half = BLK // 2
    lane = lax.broadcasted_iota(jnp.int32, (half, LANES), 1)
    even_row = 2 * lax.broadcasted_iota(jnp.int32, (half, LANES), 0)
    for (row, q), first in FIRST.items():
        slot = 2 * q - row + HALF
        even, odd = even_odd_rows(load_block(x_ref, row, slot), load_block(x_ref, row, slot + 1))
        if q == row // 2:
            lent_even = load_block(x_ref, row + 1, HALF)
            lent_odd = pltpu.roll(lent_even, BLK, 1)
            low = lane < BLK
            even = jnp.where(low & (even_row > lane), lent_even, even)
            odd = jnp.where(low & (even_row + 1 > lane), lent_odd, odd)
            diagonal = jnp.where(even_row == lane, lent_even, 0.0) + jnp.where(even_row + 1 == lane, lent_odd, 0.0)
            out_ref[DIAGONALS + q : DIAGONALS + q + 1, :] = jnp.sum(diagonal, 0, keepdims=True)
        out_ref[pl.ds(first, half, stride=2), :] = even
        out_ref[pl.ds(first + 1, half, stride=2), :] = odd
    out_ref[DIAGONALS + TILES :, :] = jnp.zeros((8 - TILES, LANES), F32)


def unpack_split(rec_ref, hi_ref, lo_ref):
    lane = lax.broadcasted_iota(jnp.int32, (BLK, LANES), 1)
    line = lax.broadcasted_iota(jnp.int32, (BLK, LANES), 0)
    low = lane < BLK
    for p in range(TILES):
        for q in range(p, TILES):
            here = (slice(p * LANES, (p + 1) * LANES), slice(q * LANES, (q + 1) * LANES))
            there = (here[1], here[0])
            top = rec_ref[FIRST[2 * p, q] : FIRST[2 * p, q] + BLK, :]
            if p == q:
                turned = jnp.concatenate([top, top], 0).T
                upper = jnp.where(low & (line > lane), turned[:BLK], top)
                diagonal = jnp.broadcast_to(rec_ref[DIAGONALS + q : DIAGONALS + q + 1, :], (BLK, LANES))
                lent = jnp.where(line > lane, top, jnp.where(line < lane, turned[:BLK], diagonal))
                lower = jnp.where(low, turned[BLK:], pltpu.roll(lent, BLK, 1))
                hi_ref[here], lo_ref[here] = split(jnp.concatenate([upper, lower], 0))
            else:
                bottom = rec_ref[FIRST[2 * p + 1, q] : FIRST[2 * p + 1, q] + BLK, :]
                tile = jnp.concatenate([top, bottom], 0)
                hi_ref[here], lo_ref[here] = split(tile)
                hi_ref[there], lo_ref[there] = split(tile.T)


def local_kernel(pat_ref, x_ref, xh_ref, xl_ref, th_ref, tl_ref, base_ref, part_ref, side_ref, nat_ref, sqh_ref, sql_ref):
    for row in range(ROWS):
        for tile in range(3 * TILES):
            slot = 2 * tile - row
            store_pair(nat_ref, (tile,), row * BLK, load_block(x_ref, row, slot), load_block(x_ref, row, slot + 1))
    for tile in range(3 * TILES):
        cols = slice(tile * LANES, (tile + 1) * LANES)
        xh_ref[:, cols], xl_ref[:, cols] = split(nat_ref[tile])
        th_ref[cols, :], tl_ref[cols, :] = split(nat_ref[tile].T)
    square = dot3(xh_ref[...], xl_ref[...], th_ref[...], tl_ref[...])
    for row in range(ROWS):
        rows = slice(row * BLK, (row + 1) * BLK)
        for tile in range(TILES):
            cols = slice(tile * LANES, (tile + 1) * LANES)
            kept = square[rows, cols] * mask_tile(pat_ref, row, TILES + tile)
            base_ref[rows, cols] = kept
            sqh_ref[rows, cols], sql_ref[rows, cols] = split(kept)
    dh, dl = xh_ref[:, SUP : 2 * SUP], xl_ref[:, SUP : 2 * SUP]
    for side, first in ((0, 0), (1, 2 * SUP)):
        cols = slice(first, first + SUP)
        part_ref[side] = dot3(dh, dl, xh_ref[:, cols], xl_ref[:, cols])
        side_ref[side] = dot3(sqh_ref[...], sql_ref[...], xh_ref[:, cols], xl_ref[:, cols])
    cube = dot3(sqh_ref[...], sql_ref[...], dh, dl)
    base_ref[...] = 3.0 * base_ref[...] - 2.0 * cube


def corner_product(side, ah, al, bh, bl):
    wide, narrow = ((0, 2), (2, 3)) if side else ((1, 3), (0, 1))
    (w0, w1), (n0, n1) = (tuple(LANES * t for t in span) for span in (wide, narrow))
    w, n = slice(w0, w1), slice(n0, n1)
    main = dot3(ah[:, w], al[:, w], bh[w, w], bl[w, w])
    extra = dot3(ah[n, n], al[n, n], bh[n, w], bl[n, w])
    own = dot3(ah[n, :], al[n, :], bh[:, n], bl[:, n])
    return main, extra, own


def corner_tile(side, parts, p, t):
    main, extra, own = parts
    if (t > p) if side else (t < p):
        return None
    far = TILES - 1 if side else 0
    rows = slice(p * LANES, (p + 1) * LANES)
    if t == far:
        return own
    base = 0 if side else 1
    lanes = slice((t - base) * LANES, (t - base + 1) * LANES)
    if p == far:
        return main[rows, lanes] + extra[:, lanes]
    return main[rows, lanes]


def finish_kernel(
    pat_ref, prev_ref, next_ref, xh_ref, xl_ref, th_ref, tl_ref, base_ref, part_ref, side_ref,
    out_hbm, dh_ref, dl_ref, eh_ref, el_ref, nat_ref, out_ref, sems,
):
    for side, rec_ref in ((0, prev_ref), (1, next_ref)):
        unpack_split(rec_ref, dh_ref.at[side], dl_ref.at[side])
    for side in (0, 1):
        cols = slice(2 * side * SUP, (2 * side + 1) * SUP)
        parts = corner_product(side, xh_ref[:, cols], xl_ref[:, cols], dh_ref[side], dl_ref[side])
        for p in range(TILES):
            for t in range(TILES):
                edge = corner_tile(side, parts, p, t)
                lanes = slice(side * SUP + t * LANES, side * SUP + (t + 1) * LANES)
                tile = 2 * side * TILES + t
                if edge is None:
                    nothing = jnp.zeros((LANES, LANES), BF16)
                    eh_ref[p * LANES : (p + 1) * LANES, lanes] = nothing
                    el_ref[p * LANES : (p + 1) * LANES, lanes] = nothing
                    continue
                edge = edge + part_ref[side, p * LANES : (p + 1) * LANES, t * LANES : (t + 1) * LANES]
                for row in (2 * p, 2 * p + 1):
                    rows = slice(row * BLK, (row + 1) * BLK)
                    kept = edge[row % 2 * BLK : (row % 2 + 1) * BLK] * mask_tile(pat_ref, row, tile)
                    nat_ref[tile, rows, :] = 3.0 * kept
                    eh_ref[rows, lanes], el_ref[rows, lanes] = split(kept)
    wide0, narrow0 = slice(LANES, SUP), slice(0, LANES)
    wide1, narrow1 = slice(0, 2 * LANES), slice(2 * LANES, SUP)
    eh, el = (ref[:, :SUP] for ref in (eh_ref, el_ref))
    fh, fl = (ref[:, SUP:] for ref in (eh_ref, el_ref))
    lh, ll = (ref[:SUP, :] for ref in (th_ref, tl_ref))
    uh, ul = (ref[2 * SUP :, :] for ref in (th_ref, tl_ref))
    main = dot3(
        jnp.concatenate([eh[:, wide0], fh[:, wide1]], 1),
        jnp.concatenate([el[:, wide0], fl[:, wide1]], 1),
        jnp.concatenate([lh[wide0, :], uh[wide1, :]], 0),
        jnp.concatenate([ll[wide0, :], ul[wide1, :]], 0),
    )
    first = dot3(eh[narrow0, narrow0], el[narrow0, narrow0], lh[narrow0, narrow0], ll[narrow0, narrow0])
    last = dot3(fh[narrow1, narrow1], fl[narrow1, narrow1], uh[narrow1, narrow1], ul[narrow1, narrow1])
    for p in range(TILES):
        rows = slice(p * LANES, (p + 1) * LANES)
        for t in range(TILES):
            lanes = slice(t * LANES, (t + 1) * LANES)
            cube = main[rows, lanes]
            if p == t == 0:
                cube = cube + first
            if p == t == TILES - 1:
                cube = cube + last
            nat_ref[TILES + t, rows, :] = base_ref[rows, lanes] - 2.0 * cube
    for side in (0, 1):
        cols = slice(side * SUP, (side + 1) * SUP)
        parts = corner_product(side, eh_ref[:, cols], el_ref[:, cols], dh_ref[side], dl_ref[side])
        for p in range(TILES):
            rows = slice(p * LANES, (p + 1) * LANES)
            for t in range(TILES):
                cube = corner_tile(side, parts, p, t)
                if cube is None:
                    continue
                tile = 2 * side * TILES + t
                cube = cube + side_ref[side, rows, t * LANES : (t + 1) * LANES]
                nat_ref[tile, rows, :] = nat_ref[tile, rows, :] - 2.0 * cube
    copies = []
    for row in range(ROWS):
        for tile in range(row // 2, (row + SLOTS - 1) // 2 + 1):
            mask = mask_tile(pat_ref, row, tile)
            even = nat_ref[tile, pl.ds(row * BLK, BLK // 2, stride=2), :] * mask
            odd = nat_ref[tile, pl.ds(row * BLK + 1, BLK // 2, stride=2), :] * mask
            left, right = even_odd_rows(even, odd)
            for slot, block in ((2 * tile - row, left), (2 * tile + 1 - row, right)):
                if 0 <= slot < SLOTS:
                    out_ref[row, slot, :] = block.reshape(BLK * BLK)
        copies.append(pltpu.make_async_copy(out_ref.at[row], out_hbm.at[row], sems.at[row]))
        copies[-1].start()
    for copy in copies:
        copy.wait()


def from_behind(x, by):
    axes = ("row", "col")
    length = lax.axis_size(axes)
    return lax.ppermute(x, axes, [(i, (i + by) % length) for i in range(length)])


def on_chip(x):
    return pltpu.with_memory_space_constraint(x, pltpu.VMEM)


def shards(density, pattern):
    smem = pl.BlockSpec(memory_space=pltpu.SMEM)
    vmem = pl.BlockSpec(memory_space=pltpu.VMEM)
    packed, density = pl.pallas_call(
        pack_kernel,
        name="pack",
        compiler_params=SMALL,
        in_specs=[pl.BlockSpec(memory_space=pltpu.HBM)],
        out_specs=[vmem] * 2,
        out_shape=[pltpu.VMEM((PACKED, LANES), F32), pltpu.VMEM((ROWS, SLOTS, BLK * BLK), F32)],
        scratch_shapes=[pltpu.SemaphoreType.DMA((ROWS,))],
    )(pltpu.with_memory_space_constraint(density, pltpu.HBM))
    density = on_chip(density)
    following = from_behind(packed, -1)
    prev = from_behind(packed, 1)
    local = pl.pallas_call(
        local_kernel,
        name="local",
        compiler_params=SMALL,
        in_specs=[smem, vmem],
        out_specs=[vmem] * 7,
        out_shape=[
            pltpu.VMEM((SUP, 3 * SUP), BF16),
            pltpu.VMEM((SUP, 3 * SUP), BF16),
            pltpu.VMEM((3 * SUP, SUP), BF16),
            pltpu.VMEM((3 * SUP, SUP), BF16),
            pltpu.VMEM((SUP, SUP), F32),
            pltpu.VMEM((2, SUP, SUP), F32),
            pltpu.VMEM((2, SUP, SUP), F32),
        ],
        scratch_shapes=[
            pltpu.VMEM((3 * TILES, SUP, LANES), F32),
            pltpu.VMEM((SUP, SUP), BF16),
            pltpu.VMEM((SUP, SUP), BF16),
        ],
    )(pattern, density)
    return pl.pallas_call(
        finish_kernel,
        name="finish",
        compiler_params=SMALL,
        in_specs=[smem] + [vmem] * 9,
        out_specs=pl.BlockSpec(memory_space=pltpu.HBM),
        out_shape=jax.ShapeDtypeStruct((ROWS, SLOTS, BLK * BLK), F32),
        scratch_shapes=[
            pltpu.VMEM((2, SUP, SUP), BF16),
            pltpu.VMEM((2, SUP, SUP), BF16),
            pltpu.VMEM((SUP, 2 * SUP), BF16),
            pltpu.VMEM((SUP, 2 * SUP), BF16),
            pltpu.VMEM((3 * TILES, SUP, LANES), F32),
            pltpu.VMEM((ROWS, SLOTS, BLK * BLK), F32),
            pltpu.SemaphoreType.DMA((ROWS,)),
        ],
    )(pattern, *(on_chip(x) for x in (prev, following, *local)))


def solution(mesh):
    return jax.shard_map(
        shards,
        mesh=mesh,
        in_specs=(P(("row", "col"), None, None), P(("row", "col"), None)),
        out_specs=P(("row", "col"), None, None),
        check_vma=False,
    )
```

```python
import jax
import jax.numpy as jnp
from jax import lax
from jax.experimental import pallas as pl
from jax.experimental.pallas import tpu as pltpu
from jax.sharding import PartitionSpec as P


BLK = 64
HALF = 6
SLOTS = 13
ROWS = 6
SUP = ROWS * BLK
LANES = 128
TILES = SUP // LANES
F32 = jnp.float32
BF16 = jnp.bfloat16
SMALL = pltpu.CompilerParams(vmem_limit_bytes=24 << 20)


def lane_is_low(rows):
    return lax.broadcasted_iota(jnp.int32, (rows, LANES), 1) < BLK


def load_block(x_ref, row, slot):
    if slot < 0 or slot >= SLOTS:
        return jnp.zeros((BLK // 2, LANES), F32)
    return x_ref[row, slot, :].reshape(BLK // 2, LANES)


def even_odd_rows(left, right):
    low = lane_is_low(BLK // 2)
    even = jnp.where(low, left, pltpu.roll(right, BLK, 1))
    odd = jnp.where(low, pltpu.roll(left, BLK, 1), right)
    return even, odd


def store_pair(ref, lead, first_row, left, right):
    even, odd = even_odd_rows(left, right)
    ref[(*lead, pl.ds(first_row, BLK // 2, stride=2), slice(None))] = even
    ref[(*lead, pl.ds(first_row + 1, BLK // 2, stride=2), slice(None))] = odd


def split(x):
    hi = x.astype(BF16)
    return hi, (x - hi.astype(F32)).astype(BF16)


def dot(a, b):
    return jnp.dot(a, b, preferred_element_type=F32)


def dot3(ah, al, bh, bl):
    return dot(jnp.concatenate([ah, ah, al], 1), jnp.concatenate([bh, bl, bh], 0))


def mask_tile(pat_ref, row, tile):
    values = []
    for q in (2 * tile, 2 * tile + 1):
        slot = q - row
        values.append(pat_ref[row, slot].astype(F32) if 0 <= slot < SLOTS else jnp.float32(0.0))
    return jnp.where(lane_is_low(8), values[0], values[1])[:1]


def packed_rows():
    first = {}
    for p in range(TILES):
        for row in (2 * p, 2 * p + 1):
            for q in range(p + row % 2, TILES):
                first[row, q] = BLK * len(first)
    return first


FIRST = packed_rows()
DIAGONALS = BLK * len(FIRST)
PACKED = DIAGONALS + 8


def pack_kernel(hbm_ref, out_ref, x_ref, sems):
    copies = [pltpu.make_async_copy(hbm_ref.at[row], x_ref.at[row], sems.at[row]) for row in range(ROWS)]
    for copy in copies:
        copy.start()
    for copy in copies:
        copy.wait()
    half = BLK // 2
    lane = lax.broadcasted_iota(jnp.int32, (half, LANES), 1)
    even_row = 2 * lax.broadcasted_iota(jnp.int32, (half, LANES), 0)
    for (row, q), first in FIRST.items():
        slot = 2 * q - row + HALF
        even, odd = even_odd_rows(load_block(x_ref, row, slot), load_block(x_ref, row, slot + 1))
        if q == row // 2:
            lent_even = load_block(x_ref, row + 1, HALF)
            lent_odd = pltpu.roll(lent_even, BLK, 1)
            low = lane < BLK
            even = jnp.where(low & (even_row > lane), lent_even, even)
            odd = jnp.where(low & (even_row + 1 > lane), lent_odd, odd)
            diagonal = jnp.where(even_row == lane, lent_even, 0.0) + jnp.where(even_row + 1 == lane, lent_odd, 0.0)
            out_ref[DIAGONALS + q : DIAGONALS + q + 1, :] = jnp.sum(diagonal, 0, keepdims=True)
        out_ref[pl.ds(first, half, stride=2), :] = even
        out_ref[pl.ds(first + 1, half, stride=2), :] = odd
    out_ref[DIAGONALS + TILES :, :] = jnp.zeros((8 - TILES, LANES), F32)


def unpack_split(rec_ref, hi_ref, lo_ref):
    lane = lax.broadcasted_iota(jnp.int32, (BLK, LANES), 1)
    line = lax.broadcasted_iota(jnp.int32, (BLK, LANES), 0)
    low = lane < BLK
    for p in range(TILES):
        for q in range(p, TILES):
            here = (slice(p * LANES, (p + 1) * LANES), slice(q * LANES, (q + 1) * LANES))
            there = (here[1], here[0])
            top = rec_ref[FIRST[2 * p, q] : FIRST[2 * p, q] + BLK, :]
            if p == q:
                turned = jnp.concatenate([top, top], 0).T
                upper = jnp.where(low & (line > lane), turned[:BLK], top)
                diagonal = jnp.broadcast_to(rec_ref[DIAGONALS + q : DIAGONALS + q + 1, :], (BLK, LANES))
                lent = jnp.where(line > lane, top, jnp.where(line < lane, turned[:BLK], diagonal))
                lower = jnp.where(low, turned[BLK:], pltpu.roll(lent, BLK, 1))
                hi_ref[here], lo_ref[here] = split(jnp.concatenate([upper, lower], 0))
            else:
                bottom = rec_ref[FIRST[2 * p + 1, q] : FIRST[2 * p + 1, q] + BLK, :]
                tile = jnp.concatenate([top, bottom], 0)
                hi_ref[here], lo_ref[here] = split(tile)
                hi_ref[there], lo_ref[there] = split(tile.T)


def spans(side):
    if side:
        return slice(0, 2 * LANES), slice(2 * LANES, SUP)
    return slice(LANES, SUP), slice(0, LANES)


def panel_product(side, out_ref, ah, al, bh, bl):
    w, n = spans(side)
    out_ref[:, w] = dot3(ah, al, bh[:, w], bl[:, w])
    out_ref[n, n] = dot3(ah[n, n], al[n, n], bh[n, n], bl[n, n])


def local_kernel(pat_ref, x_ref, xh_ref, xl_ref, th_ref, tl_ref, base_ref, part_ref, side_ref, nat_ref, sqh_ref, sql_ref):
    for row in range(ROWS):
        for tile in range(3 * TILES):
            slot = 2 * tile - row
            store_pair(nat_ref, (tile,), row * BLK, load_block(x_ref, row, slot), load_block(x_ref, row, slot + 1))
    for tile in range(3 * TILES):
        cols = slice(tile * LANES, (tile + 1) * LANES)
        xh_ref[:, cols], xl_ref[:, cols] = split(nat_ref[tile])
        th_ref[cols, :], tl_ref[cols, :] = split(nat_ref[tile].T)
    wide, last, used = slice(0, 2 * LANES), slice(2 * LANES, SUP), slice(2 * LANES, 3 * SUP)
    main = dot3(xh_ref[...], xl_ref[...], th_ref[:, wide], tl_ref[:, wide])
    own = dot3(xh_ref[last, used], xl_ref[last, used], th_ref[used, last], tl_ref[used, last])
    for p in range(TILES):
        for t in range(TILES):
            cols = slice(t * LANES, (t + 1) * LANES)
            if t < TILES - 1:
                square = main[p * LANES : (p + 1) * LANES, cols]
            else:
                square = own if p == t else main[last, p * LANES : (p + 1) * LANES].T
            for row in (2 * p, 2 * p + 1):
                rows = slice(row * BLK, (row + 1) * BLK)
                kept = square[row % 2 * BLK : (row % 2 + 1) * BLK] * mask_tile(pat_ref, row, TILES + t)
                base_ref[rows, cols] = kept
                sqh_ref[rows, cols], sql_ref[rows, cols] = split(kept)
    dh, dl = xh_ref[:, SUP : 2 * SUP], xl_ref[:, SUP : 2 * SUP]
    for side, first in ((0, 0), (1, 2 * SUP)):
        cols = slice(first, first + SUP)
        panel_product(side, part_ref.at[side], dh, dl, xh_ref[:, cols], xl_ref[:, cols])
        panel_product(side, side_ref.at[side], sqh_ref[...], sql_ref[...], xh_ref[:, cols], xl_ref[:, cols])
    cube = dot3(sqh_ref[...], sql_ref[...], dh, dl)
    base_ref[...] = 3.0 * base_ref[...] - 2.0 * cube


def corner_product(side, ah, al, bh, bl):
    w, n = spans(side)
    main = dot3(ah[:, w], al[:, w], bh[w, w], bl[w, w])
    extra = dot3(ah[n, n], al[n, n], bh[n, w], bl[n, w])
    own = dot3(ah[n, :], al[n, :], bh[:, n], bl[:, n])
    return main, extra, own


def corner_tile(side, parts, p, t):
    main, extra, own = parts
    if (t > p) if side else (t < p):
        return None
    far = TILES - 1 if side else 0
    rows = slice(p * LANES, (p + 1) * LANES)
    if t == far:
        return own
    base = 0 if side else 1
    lanes = slice((t - base) * LANES, (t - base + 1) * LANES)
    if p == far:
        return main[rows, lanes] + extra[:, lanes]
    return main[rows, lanes]


def one_side(side, pat_ref, rec_ref, x_refs, t_refs, base_ref, part_ref, side_ref, nat_ref, sum_ref, d_refs, e_refs):
    (xh_ref, xl_ref), (th_ref, tl_ref), (dh_ref, dl_ref), (eh_ref, el_ref) = x_refs, t_refs, d_refs, e_refs
    unpack_split(rec_ref, dh_ref, dl_ref)
    panel = slice(2 * side * SUP, (2 * side + 1) * SUP)
    far = TILES - 1 if side else 0
    parts = corner_product(side, xh_ref[:, panel], xl_ref[:, panel], dh_ref, dl_ref)
    for p in range(TILES):
        rows = slice(p * LANES, (p + 1) * LANES)
        for t in range(TILES):
            edge = corner_tile(side, parts, p, t)
            lanes = slice(t * LANES, (t + 1) * LANES)
            if edge is None:
                nothing = jnp.zeros((LANES, LANES), BF16)
                eh_ref[rows, lanes], el_ref[rows, lanes] = nothing, nothing
                nat_ref[t, rows, :] = jnp.zeros((LANES, LANES), F32)
                continue
            edge = edge + part_ref[side, rows, lanes]
            for row in (2 * p, 2 * p + 1):
                half = slice(row * BLK, (row + 1) * BLK)
                kept = edge[row % 2 * BLK : (row % 2 + 1) * BLK] * mask_tile(pat_ref, row, 2 * side * TILES + t)
                nat_ref[t, half, :] = 3.0 * kept
                eh_ref[half, lanes], el_ref[half, lanes] = split(kept)
    w, n = spans(side)
    bh, bl = th_ref[panel, :], tl_ref[panel, :]
    main = dot3(eh_ref[:, w], el_ref[:, w], bh[w, :], bl[w, :])
    own = dot3(eh_ref[n, n], el_ref[n, n], bh[n, n], bl[n, n])
    for p in range(TILES):
        rows = slice(p * LANES, (p + 1) * LANES)
        for t in range(TILES):
            lanes = slice(t * LANES, (t + 1) * LANES)
            cube = main[rows, lanes]
            if p == t == far:
                cube = cube + own
            sum_ref[rows, lanes] = base_ref[rows, lanes] - 2.0 * cube
    parts = corner_product(side, eh_ref, el_ref, dh_ref, dl_ref)
    for p in range(TILES):
        rows = slice(p * LANES, (p + 1) * LANES)
        for t in range(TILES):
            cube = corner_tile(side, parts, p, t)
            if cube is not None:
                cube = cube + side_ref[side, rows, t * LANES : (t + 1) * LANES]
                nat_ref[t, rows, :] = nat_ref[t, rows, :] - 2.0 * cube


def next_kernel(
    pat_ref, rec_ref, xh_ref, xl_ref, th_ref, tl_ref, base_ref, part_ref, side_ref,
    nat_ref, sum_ref, dh_ref, dl_ref, eh_ref, el_ref,
):
    one_side(
        1, pat_ref, rec_ref, (xh_ref, xl_ref), (th_ref, tl_ref), base_ref, part_ref, side_ref,
        nat_ref, sum_ref, (dh_ref, dl_ref), (eh_ref, el_ref),
    )


def prev_kernel(
    pat_ref, rec_ref, xh_ref, xl_ref, th_ref, tl_ref, base_ref, part_ref, side_ref, right_ref,
    out_hbm, left_ref, sum_ref, mid_ref, dh_ref, dl_ref, eh_ref, el_ref, out_ref, sems,
):
    one_side(
        0, pat_ref, rec_ref, (xh_ref, xl_ref), (th_ref, tl_ref), base_ref, part_ref, side_ref,
        left_ref, sum_ref, (dh_ref, dl_ref), (eh_ref, el_ref),
    )
    for t in range(TILES):
        mid_ref[t] = sum_ref[:, t * LANES : (t + 1) * LANES]
    copies = []
    for row in range(ROWS):
        for tile in range(row // 2, (row + SLOTS - 1) // 2 + 1):
            nat_ref = (left_ref, mid_ref, right_ref)[tile // TILES]
            mask = mask_tile(pat_ref, row, tile)
            even = nat_ref[tile % TILES, pl.ds(row * BLK, BLK // 2, stride=2), :] * mask
            odd = nat_ref[tile % TILES, pl.ds(row * BLK + 1, BLK // 2, stride=2), :] * mask
            left, right = even_odd_rows(even, odd)
            for slot, block in ((2 * tile - row, left), (2 * tile + 1 - row, right)):
                if 0 <= slot < SLOTS:
                    out_ref[row, slot, :] = block.reshape(BLK * BLK)
        copies.append(pltpu.make_async_copy(out_ref.at[row], out_hbm.at[row], sems.at[row]))
        copies[-1].start()
    for copy in copies:
        copy.wait()


def from_behind(x, by):
    axes = ("row", "col")
    length = lax.axis_size(axes)
    return lax.ppermute(x, axes, [(i, (i + by) % length) for i in range(length)])


def on_chip(x):
    return pltpu.with_memory_space_constraint(x, pltpu.VMEM)


def shards(density, pattern):
    smem = pl.BlockSpec(memory_space=pltpu.SMEM)
    vmem = pl.BlockSpec(memory_space=pltpu.VMEM)
    packed, density = pl.pallas_call(
        pack_kernel,
        name="pack",
        compiler_params=SMALL,
        in_specs=[pl.BlockSpec(memory_space=pltpu.HBM)],
        out_specs=[vmem] * 2,
        out_shape=[pltpu.VMEM((PACKED, LANES), F32), pltpu.VMEM((ROWS, SLOTS, BLK * BLK), F32)],
        scratch_shapes=[pltpu.SemaphoreType.DMA((ROWS,))],
    )(pltpu.with_memory_space_constraint(density, pltpu.HBM))
    density = on_chip(density)
    prev = from_behind(packed, 1)
    following = from_behind(packed, -1)
    local = pl.pallas_call(
        local_kernel,
        name="local",
        compiler_params=SMALL,
        in_specs=[smem, vmem],
        out_specs=[vmem] * 7,
        out_shape=[
            pltpu.VMEM((SUP, 3 * SUP), BF16),
            pltpu.VMEM((SUP, 3 * SUP), BF16),
            pltpu.VMEM((3 * SUP, SUP), BF16),
            pltpu.VMEM((3 * SUP, SUP), BF16),
            pltpu.VMEM((SUP, SUP), F32),
            pltpu.VMEM((2, SUP, SUP), F32),
            pltpu.VMEM((2, SUP, SUP), F32),
        ],
        scratch_shapes=[
            pltpu.VMEM((3 * TILES, SUP, LANES), F32),
            pltpu.VMEM((SUP, SUP), BF16),
            pltpu.VMEM((SUP, SUP), BF16),
        ],
    )(pattern, density)
    *x_and_t, base, part, side = (on_chip(x) for x in local)
    work = [pltpu.VMEM((SUP, SUP), BF16) for _ in range(4)]
    strip = (TILES, SUP, LANES)
    right, base = pl.pallas_call(
        next_kernel,
        name="next_side",
        compiler_params=SMALL,
        in_specs=[smem] + [vmem] * 8,
        out_specs=[vmem] * 2,
        out_shape=[pltpu.VMEM(strip, F32), pltpu.VMEM((SUP, SUP), F32)],
        scratch_shapes=work,
    )(pattern, on_chip(following), *x_and_t, base, part, side)
    return pl.pallas_call(
        prev_kernel,
        name="prev_side",
        compiler_params=SMALL,
        in_specs=[smem] + [vmem] * 9,
        out_specs=pl.BlockSpec(memory_space=pltpu.HBM),
        out_shape=jax.ShapeDtypeStruct((ROWS, SLOTS, BLK * BLK), F32),
        scratch_shapes=[
            pltpu.VMEM(strip, F32),
            pltpu.VMEM((SUP, SUP), F32),
            pltpu.VMEM(strip, F32),
            *work,
            pltpu.VMEM((ROWS, SLOTS, BLK * BLK), F32),
            pltpu.SemaphoreType.DMA((ROWS,)),
        ],
    )(pattern, on_chip(prev), *x_and_t, on_chip(base), part, side, on_chip(right))


def solution(mesh):
    return jax.shard_map(
        shards,
        mesh=mesh,
        in_specs=(P(("row", "col"), None, None), P(("row", "col"), None)),
        out_specs=P(("row", "col"), None, None),
        check_vma=False,
    )
```

```python
import jax
import jax.numpy as jnp
from jax import lax
from jax.experimental import pallas as pl
from jax.experimental.pallas import tpu as pltpu
from jax.sharding import PartitionSpec as P

BLK = 64
HALF = 6
SLOTS = 13
ROWS = 6
SUP = ROWS * BLK
LANES = 128
TILES = SUP // LANES
F32 = jnp.float32
BF16 = jnp.bfloat16
SMALL = pltpu.CompilerParams(vmem_limit_bytes=24 << 20)


def lane_is_low(rows):
    return lax.broadcasted_iota(jnp.int32, (rows, LANES), 1) < BLK


def load_block(x_ref, row, slot):
    if slot < 0 or slot >= SLOTS:
        return jnp.zeros((BLK // 2, LANES), F32)
    return x_ref[row, slot, :].reshape(BLK // 2, LANES)


def even_odd_rows(left, right):
    low = lane_is_low(BLK // 2)
    even = jnp.where(low, left, pltpu.roll(right, BLK, 1))
    odd = jnp.where(low, pltpu.roll(left, BLK, 1), right)
    return even, odd


def store_pair(ref, lead, first_row, left, right):
    even, odd = even_odd_rows(left, right)
    ref[(*lead, pl.ds(first_row, BLK // 2, stride=2), slice(None))] = even
    ref[(*lead, pl.ds(first_row + 1, BLK // 2, stride=2), slice(None))] = odd


def split(x):
    hi = x.astype(BF16)
    return hi, (x - hi.astype(F32)).astype(BF16)


def dot(a, b):
    return jnp.dot(a, b, preferred_element_type=F32)


def dot3(ah, al, bh, bl):
    return dot(jnp.concatenate([ah, ah, al], 1), jnp.concatenate([bh, bl, bh], 0))


def mask_tile(pat_ref, row, tile):
    values = []
    for q in (2 * tile, 2 * tile + 1):
        slot = q - row
        values.append(pat_ref[row, slot].astype(F32) if 0 <= slot < SLOTS else jnp.float32(0.0))
    return jnp.where(lane_is_low(8), values[0], values[1])[:1]


def packed_rows():
    first = {}
    for p in range(TILES):
        for row in (2 * p, 2 * p + 1):
            for q in range(p + row % 2, TILES):
                first[row, q] = BLK * len(first)
    return first


FIRST = packed_rows()
DIAGONALS = BLK * len(FIRST)
PACKED = DIAGONALS + 8


def pack_kernel(hbm_ref, out_ref, x_ref, sems):
    copies = [pltpu.make_async_copy(hbm_ref.at[row], x_ref.at[row], sems.at[row]) for row in range(ROWS)]
    for copy in copies:
        copy.start()
    for copy in copies:
        copy.wait()
    half = BLK // 2
    lane = lax.broadcasted_iota(jnp.int32, (half, LANES), 1)
    even_row = 2 * lax.broadcasted_iota(jnp.int32, (half, LANES), 0)
    for (row, q), first in FIRST.items():
        slot = 2 * q - row + HALF
        even, odd = even_odd_rows(load_block(x_ref, row, slot), load_block(x_ref, row, slot + 1))
        if q == row // 2:
            lent_even = load_block(x_ref, row + 1, HALF)
            lent_odd = pltpu.roll(lent_even, BLK, 1)
            low = lane < BLK
            even = jnp.where(low & (even_row > lane), lent_even, even)
            odd = jnp.where(low & (even_row + 1 > lane), lent_odd, odd)
            diagonal = jnp.where(even_row == lane, lent_even, 0.0) + jnp.where(even_row + 1 == lane, lent_odd, 0.0)
            out_ref[DIAGONALS + q : DIAGONALS + q + 1, :] = jnp.sum(diagonal, 0, keepdims=True)
        out_ref[pl.ds(first, half, stride=2), :] = even
        out_ref[pl.ds(first + 1, half, stride=2), :] = odd
    out_ref[DIAGONALS + TILES :, :] = jnp.zeros((8 - TILES, LANES), F32)


def unpack_split(rec_ref, hi_ref, lo_ref):
    lane = lax.broadcasted_iota(jnp.int32, (BLK, LANES), 1)
    line = lax.broadcasted_iota(jnp.int32, (BLK, LANES), 0)
    low = lane < BLK
    for p in range(TILES):
        for q in range(p, TILES):
            here = (slice(p * LANES, (p + 1) * LANES), slice(q * LANES, (q + 1) * LANES))
            there = (here[1], here[0])
            top = rec_ref[FIRST[2 * p, q] : FIRST[2 * p, q] + BLK, :]
            if p == q:
                turned = jnp.concatenate([top, top], 0).T
                upper = jnp.where(low & (line > lane), turned[:BLK], top)
                diagonal = jnp.broadcast_to(rec_ref[DIAGONALS + q : DIAGONALS + q + 1, :], (BLK, LANES))
                lent = jnp.where(line > lane, top, jnp.where(line < lane, turned[:BLK], diagonal))
                lower = jnp.where(low, turned[BLK:], pltpu.roll(lent, BLK, 1))
                hi_ref[here], lo_ref[here] = split(jnp.concatenate([upper, lower], 0))
            else:
                bottom = rec_ref[FIRST[2 * p + 1, q] : FIRST[2 * p + 1, q] + BLK, :]
                tile = jnp.concatenate([top, bottom], 0)
                hi_ref[here], lo_ref[here] = split(tile)
                hi_ref[there], lo_ref[there] = split(tile.T)


def spans(side):
    if side:
        return slice(0, 2 * LANES), slice(2 * LANES, SUP)
    return slice(LANES, SUP), slice(0, LANES)


def panel_product(side, out_ref, ah, al, bh, bl):
    w, n = spans(side)
    out_ref[:, w] = dot3(ah, al, bh[:, w], bl[:, w])
    out_ref[n, n] = dot3(ah[n, n], al[n, n], bh[n, n], bl[n, n])


def local_kernel(pat_ref, x_ref, xh_ref, xl_ref, th_ref, tl_ref, base_ref, part_ref, side_ref, nat_ref, sqh_ref, sql_ref):
    for row in range(ROWS):
        for tile in range(3 * TILES):
            slot = 2 * tile - row
            store_pair(nat_ref, (tile,), row * BLK, load_block(x_ref, row, slot), load_block(x_ref, row, slot + 1))
    for tile in range(3 * TILES):
        cols = slice(tile * LANES, (tile + 1) * LANES)
        xh_ref[:, cols], xl_ref[:, cols] = split(nat_ref[tile])
        th_ref[cols, :], tl_ref[cols, :] = split(nat_ref[tile].T)
    wide, last, used = slice(0, 2 * LANES), slice(2 * LANES, SUP), slice(2 * LANES, 3 * SUP)
    main = dot3(xh_ref[...], xl_ref[...], th_ref[:, wide], tl_ref[:, wide])
    own = dot3(xh_ref[last, used], xl_ref[last, used], th_ref[used, last], tl_ref[used, last])
    for p in range(TILES):
        for t in range(TILES):
            cols = slice(t * LANES, (t + 1) * LANES)
            if t < TILES - 1:
                square = main[p * LANES : (p + 1) * LANES, cols]
            else:
                square = own if p == t else main[last, p * LANES : (p + 1) * LANES].T
            for row in (2 * p, 2 * p + 1):
                rows = slice(row * BLK, (row + 1) * BLK)
                kept = square[row % 2 * BLK : (row % 2 + 1) * BLK] * mask_tile(pat_ref, row, TILES + t)
                base_ref[rows, cols] = kept
                sqh_ref[rows, cols], sql_ref[rows, cols] = split(kept)
    dh, dl = xh_ref[:, SUP : 2 * SUP], xl_ref[:, SUP : 2 * SUP]
    for side, first in ((0, 0), (1, 2 * SUP)):
        cols = slice(first, first + SUP)
        panel_product(side, part_ref.at[side], dh, dl, xh_ref[:, cols], xl_ref[:, cols])
        panel_product(side, side_ref.at[side], sqh_ref[...], sql_ref[...], xh_ref[:, cols], xl_ref[:, cols])
    cube = dot3(sqh_ref[...], sql_ref[...], dh, dl)
    base_ref[...] = 3.0 * base_ref[...] - 2.0 * cube


def corner_product(side, ah, al, bh, bl):
    w, n = spans(side)
    main = dot3(ah[:, w], al[:, w], bh[w, w], bl[w, w])
    extra = dot3(ah[n, n], al[n, n], bh[n, w], bl[n, w])
    own = dot3(ah[n, :], al[n, :], bh[:, n], bl[:, n])
    return main, extra, own


def corner_tile(side, parts, p, t):
    main, extra, own = parts
    if (t > p) if side else (t < p):
        return None
    far = TILES - 1 if side else 0
    rows = slice(p * LANES, (p + 1) * LANES)
    if t == far:
        return own
    base = 0 if side else 1
    lanes = slice((t - base) * LANES, (t - base + 1) * LANES)
    if p == far:
        return main[rows, lanes] + extra[:, lanes]
    return main[rows, lanes]


def write_tiles(pat_ref, nat_ref, out_ref, panel):
    for row in range(ROWS):
        for tile in range(panel * TILES, (panel + 1) * TILES):
            slots = (2 * tile - row, 2 * tile + 1 - row)
            if slots[1] < 0 or slots[0] >= SLOTS:
                continue
            mask = mask_tile(pat_ref, row, tile)
            even = nat_ref[tile, pl.ds(row * BLK, BLK // 2, stride=2), :] * mask
            odd = nat_ref[tile, pl.ds(row * BLK + 1, BLK // 2, stride=2), :] * mask
            for slot, block in zip(slots, even_odd_rows(even, odd)):
                if 0 <= slot < SLOTS:
                    out_ref[row, slot, :] = block.reshape(BLK * BLK)


def finish_kernel(
    pat_ref, prev_ref, next_ref, xh_ref, xl_ref, th_ref, tl_ref, base_ref, part_ref, side_ref,
    out_hbm, dh_ref, dl_ref, eh_ref, el_ref, nat_ref, out_ref, sems,
):
    for side, rec_ref in ((0, prev_ref), (1, next_ref)):
        unpack_split(rec_ref, dh_ref.at[side], dl_ref.at[side])
    for side in (0, 1):
        cols = slice(2 * side * SUP, (2 * side + 1) * SUP)
        parts = corner_product(side, xh_ref[:, cols], xl_ref[:, cols], dh_ref[side], dl_ref[side])
        for p in range(TILES):
            for t in range(TILES):
                edge = corner_tile(side, parts, p, t)
                lanes = slice(side * SUP + t * LANES, side * SUP + (t + 1) * LANES)
                tile = 2 * side * TILES + t
                if edge is None:
                    nothing = jnp.zeros((LANES, LANES), BF16)
                    eh_ref[p * LANES : (p + 1) * LANES, lanes] = nothing
                    el_ref[p * LANES : (p + 1) * LANES, lanes] = nothing
                    continue
                edge = edge + part_ref[side, p * LANES : (p + 1) * LANES, t * LANES : (t + 1) * LANES]
                for row in (2 * p, 2 * p + 1):
                    rows = slice(row * BLK, (row + 1) * BLK)
                    kept = edge[row % 2 * BLK : (row % 2 + 1) * BLK] * mask_tile(pat_ref, row, tile)
                    nat_ref[tile, rows, :] = 3.0 * kept
                    eh_ref[rows, lanes], el_ref[rows, lanes] = split(kept)
    wide0, narrow0 = slice(LANES, SUP), slice(0, LANES)
    wide1, narrow1 = slice(0, 2 * LANES), slice(2 * LANES, SUP)
    eh, el = (ref[:, :SUP] for ref in (eh_ref, el_ref))
    fh, fl = (ref[:, SUP:] for ref in (eh_ref, el_ref))
    lh, ll = (ref[:SUP, :] for ref in (th_ref, tl_ref))
    uh, ul = (ref[2 * SUP :, :] for ref in (th_ref, tl_ref))
    main = dot3(
        jnp.concatenate([eh[:, wide0], fh[:, wide1]], 1),
        jnp.concatenate([el[:, wide0], fl[:, wide1]], 1),
        jnp.concatenate([lh[wide0, :], uh[wide1, :]], 0),
        jnp.concatenate([ll[wide0, :], ul[wide1, :]], 0),
    )
    first = dot3(eh[narrow0, narrow0], el[narrow0, narrow0], lh[narrow0, narrow0], ll[narrow0, narrow0])
    last = dot3(fh[narrow1, narrow1], fl[narrow1, narrow1], uh[narrow1, narrow1], ul[narrow1, narrow1])
    for p in range(TILES):
        rows = slice(p * LANES, (p + 1) * LANES)
        for t in range(TILES):
            lanes = slice(t * LANES, (t + 1) * LANES)
            cube = main[rows, lanes]
            if p == t == 0:
                cube = cube + first
            if p == t == TILES - 1:
                cube = cube + last
            nat_ref[TILES + t, rows, :] = base_ref[rows, lanes] - 2.0 * cube
    write_tiles(pat_ref, nat_ref, out_ref, 1)
    early = [pltpu.make_async_copy(out_ref.at[row, :8], out_hbm.at[row, :8], sems.at[row, 0]) for row in range(ROWS)]
    late = [pltpu.make_async_copy(out_ref.at[row, 8:], out_hbm.at[row, 8:], sems.at[row, 1]) for row in range(ROWS)]
    for side in (0, 1):
        cols = slice(side * SUP, (side + 1) * SUP)
        parts = corner_product(side, eh_ref[:, cols], el_ref[:, cols], dh_ref[side], dl_ref[side])
        for p in range(TILES):
            rows = slice(p * LANES, (p + 1) * LANES)
            for t in range(TILES):
                cube = corner_tile(side, parts, p, t)
                if cube is None:
                    continue
                tile = 2 * side * TILES + t
                cube = cube + side_ref[side, rows, t * LANES : (t + 1) * LANES]
                nat_ref[tile, rows, :] = nat_ref[tile, rows, :] - 2.0 * cube
        write_tiles(pat_ref, nat_ref, out_ref, 2 * side)
        if side == 0:
            for copy in early[:-1]:
                copy.start()
    for copy in (early[-1], *late):
        copy.start()
    for copy in (*early, *late):
        copy.wait()


def from_behind(x, by):
    axes = ("row", "col")
    length = lax.axis_size(axes)
    return lax.ppermute(x, axes, [(i, (i + by) % length) for i in range(length)])


def on_chip(x):
    return pltpu.with_memory_space_constraint(x, pltpu.VMEM)


def shards(density, pattern):
    smem = pl.BlockSpec(memory_space=pltpu.SMEM)
    vmem = pl.BlockSpec(memory_space=pltpu.VMEM)
    packed, density = pl.pallas_call(
        pack_kernel,
        name="pack",
        compiler_params=SMALL,
        in_specs=[pl.BlockSpec(memory_space=pltpu.HBM)],
        out_specs=[vmem] * 2,
        out_shape=[pltpu.VMEM((PACKED, LANES), F32), pltpu.VMEM((ROWS, SLOTS, BLK * BLK), F32)],
        scratch_shapes=[pltpu.SemaphoreType.DMA((ROWS,))],
    )(pltpu.with_memory_space_constraint(density, pltpu.HBM))
    density = on_chip(density)
    following = from_behind(packed, -1)
    prev = from_behind(packed, 1)
    local = pl.pallas_call(
        local_kernel,
        name="local",
        compiler_params=SMALL,
        in_specs=[smem, vmem],
        out_specs=[vmem] * 7,
        out_shape=[
            pltpu.VMEM((SUP, 3 * SUP), BF16),
            pltpu.VMEM((SUP, 3 * SUP), BF16),
            pltpu.VMEM((3 * SUP, SUP), BF16),
            pltpu.VMEM((3 * SUP, SUP), BF16),
            pltpu.VMEM((SUP, SUP), F32),
            pltpu.VMEM((2, SUP, SUP), F32),
            pltpu.VMEM((2, SUP, SUP), F32),
        ],
        scratch_shapes=[
            pltpu.VMEM((3 * TILES, SUP, LANES), F32),
            pltpu.VMEM((SUP, SUP), BF16),
            pltpu.VMEM((SUP, SUP), BF16),
        ],
    )(pattern, density)
    return pl.pallas_call(
        finish_kernel,
        name="finish",
        compiler_params=SMALL,
        in_specs=[smem] + [vmem] * 9,
        out_specs=pl.BlockSpec(memory_space=pltpu.HBM),
        out_shape=jax.ShapeDtypeStruct((ROWS, SLOTS, BLK * BLK), F32),
        scratch_shapes=[
            pltpu.VMEM((2, SUP, SUP), BF16),
            pltpu.VMEM((2, SUP, SUP), BF16),
            pltpu.VMEM((SUP, 2 * SUP), BF16),
            pltpu.VMEM((SUP, 2 * SUP), BF16),
            pltpu.VMEM((3 * TILES, SUP, LANES), F32),
            pltpu.VMEM((ROWS, SLOTS, BLK * BLK), F32),
            pltpu.SemaphoreType.DMA((ROWS, 2)),
        ],
    )(pattern, *(on_chip(x) for x in (prev, following, *local)))


def solution(mesh):
    return jax.shard_map(
        shards,
        mesh=mesh,
        in_specs=(P(("row", "col"), None, None), P(("row", "col"), None)),
        out_specs=P(("row", "col"), None, None),
        check_vma=False,
    )
```
